32 devices in a mesh: sub: 8 (over y, x, core), reg: 4 (over z).
Axes of the slice: x: 2, y: 2, z: 4, core: 2. Of those that a mesh axis runs over, the one named last changes fastest.
Arguments:
- right_side: float32 [8, 4, 1280, 16], P('sub', 'reg'), may hold values from -6 to 6
- tiles: bfloat16 [8, 4, 80, 128, 128], P('sub', 'reg'), may hold values from -1 to 5
- tile_list: int32 [8, 4, 80, 2], P('sub', 'reg'), may hold values from 0 to 9, as said below
- weights: float32 [8, 4, 1280], P('sub', 'reg'), may hold values from 0.15 to 0.35
- face_map: int32 [8, 4, 6], P('sub', 'reg'), may hold values from 0 to 9, as said below
- matching: int32 [8, 4, 6, 128], P('sub', 'reg'), may hold values from 0 to 127, each once within a row
- coarse_basis: bfloat16 [8, 4, 1280, 128], P('sub', 'reg'), may hold values from -0.15625 to 0.15625
- coarse_map: int32 [8, 4, 128], P('sub', 'reg'), may hold values from 0 to 511, as said below
- coarse_inverse: float32 [4, 512, 512], P('reg', 'sub'), may hold values from -1 to 2, as said below
Outputs:
- solution: bfloat16 [8, 4, 1280, 16], P('sub', 'reg')
- residual: bfloat16 [8, 4, 1280, 16], P('sub', 'reg')
The draws below stay inside these ranges and needn't reach their ends.
Inputs may be any that keep to these rules, and one draw needn't show every extreme that they name: `tile_list`: entries 0 to 9 of each subdomain's list are (b, b) for b in order; the other 70 entries are distinct off-diagonal block pairs. `face_map`: the six blocks of a subdomain are distinct. `coarse_map`: A subdomain's 128 numbers are distinct, and within a subregion every number is named by exactly two subdomains. `coarse_inverse`: symmetric in its last two dimensions.
All inputs are finite; a program needn't handle non-finite values.
Results may differ from the reference program's by a relative error of at most 0.0075.
Values may be sent and summed in bfloat16 or wider, within the bound.
No kernel may reach another device: no remote copies, remote signals or barrier semaphores. Data moves between devices by JAX's collectives and lax.ppermute only.
A program may use at most 64 MiB of HBM per device.

```python
import math
import jax
import jax.numpy as jnp
from jax import lax

ORDER = 1280
TILE = 128
RIGHTS = 16
COARSE = 128
SWEEPS = 3
BLOCKS = 10
LISTED = 80
SUBS = 8
REGIONS = 4
COARSE_ALL = 512
N_REG = 4


def draw_tiles(key, part):
    keys = jax.random.split(key, SUBS * REGIONS)
    spread = 0.6 / math.sqrt(ORDER)

    def single(device_key):
        first, second = jax.random.split(device_key)
        entries = jnp.clip(jax.random.normal(first, (LISTED, TILE, TILE), jnp.float32), -4.0, 4.0)
        entries = entries * spread
        diagonal = jnp.exp(jax.random.uniform(second, (BLOCKS, TILE), jnp.float32, math.log(2.0), math.log(4.0)))
        identity = jnp.eye(TILE, dtype=jnp.float32)
        entries = entries.at[:BLOCKS].add(diagonal[:, :, None] * identity[None])
        return entries.astype(jnp.bfloat16)
    return lax.map(single, keys).reshape(SUBS, REGIONS, LISTED, TILE, TILE)


def draw_tile_list(key, part):
    keys = jax.random.split(key, SUBS * REGIONS)

    def single(device_key):
        order = jax.random.permutation(device_key, BLOCKS * (BLOCKS - 1))[:LISTED - BLOCKS].astype(jnp.int32)
        rows = order // (BLOCKS - 1)
        other = order % (BLOCKS - 1)
        columns = other + (other >= rows).astype(jnp.int32)
        diagonal = jnp.arange(BLOCKS, dtype=jnp.int32)
        return jnp.stack([jnp.concatenate([diagonal, rows]), jnp.concatenate([diagonal, columns])], axis=-1)
    return jax.vmap(single)(keys).reshape(SUBS, REGIONS, LISTED, 2)


def draw_face_map(key, part):
    keys = jax.random.split(key, SUBS * REGIONS)

    def single(device_key):
        return jax.random.permutation(device_key, BLOCKS)[:6].astype(jnp.int32)
    return jax.vmap(single)(keys).reshape(SUBS, REGIONS, 6)


def draw_coarse_map(key, part):
    keys = jax.random.split(key, REGIONS)
    half = COARSE // 2

    def single(region_key):
        label_key, order_key, shift_key, shuffle_key = jax.random.split(region_key, 4)
        labels = jax.random.permutation(label_key, COARSE_ALL).astype(jnp.int32).reshape(SUBS, half)
        placing = jax.random.permutation(order_key, SUBS).astype(jnp.int32)
        ranking = jnp.zeros((SUBS,), jnp.int32).at[placing].set(jnp.arange(SUBS, dtype=jnp.int32))
        shifts = jax.random.randint(shift_key, (half,), 1, SUBS).astype(jnp.int32)
        source_rank = (ranking[:, None] - shifts[None, :]) % SUBS
        source = placing[source_rank]
        columns = jnp.broadcast_to(jnp.arange(half, dtype=jnp.int32)[None, :], (SUBS, half))
        second = labels[source, columns]
        combined = jnp.concatenate([labels, second], axis=1)
        shuffle_keys = jax.random.split(shuffle_key, SUBS)
        orders = jax.vmap(lambda one_key: jax.random.permutation(one_key, COARSE).astype(jnp.int32))(shuffle_keys)
        return jnp.take_along_axis(combined, orders, axis=1)
    return jnp.transpose(jax.vmap(single)(keys), (1, 0, 2))


def draw_coarse_inverse(key, part):
    keys = jax.random.split(key, REGIONS)

    def single(region_key):
        first, second = jax.random.split(region_key)
        raw = jnp.clip(jax.random.normal(first, (COARSE_ALL, COARSE_ALL), jnp.float32), -4.0, 4.0)
        raw = raw * (0.3 / math.sqrt(COARSE_ALL))
        symmetric = (raw + raw.T) / math.sqrt(2.0)
        diagonal = jnp.exp(jax.random.uniform(second, (COARSE_ALL,), jnp.float32, math.log(0.5), math.log(1.5)))
        return symmetric + jnp.diag(diagonal)
    return lax.map(single, keys)


def block_scale(own_key, shape, cuts, least, top_value):
    loudness = 1.0
    for position, shards_of in cuts:
        draws = jax.random.uniform(jax.random.fold_in(jax.random.fold_in(own_key, 6), position), (shards_of,), jnp.float32, least / len(cuts), top_value / len(cuts))
        loudness = loudness * jnp.repeat(jnp.exp(draws), shape[position] // shards_of).reshape((-1,) + (1,) * (len(shape) - 1 - position))
    return loudness


def scatter_about(rng, dims, width, bound, shards=(), held_as=jnp.bfloat16):
    values = width * jax.random.normal(rng, dims, jnp.float32)
    if shards:
        values = values * block_scale(rng, dims, shards, -0.22, 0.18)
    return jnp.clip(values, -bound, bound).astype(held_as)


def setup_inputs(seed: int = 0) -> dict:
    seeds = jax.random.split(jax.random.key(seed), 10)
    return {
        "right_side": scatter_about(seeds[0], (SUBS, REGIONS, ORDER, RIGHTS), 1.0, 6.0, ((0, 8), (1, 4)), jnp.float32),
        "tiles": draw_tiles(jax.random.fold_in(seeds[9], 71), 0),
        "tile_list": draw_tile_list(jax.random.fold_in(seeds[9], 71), 0),
        "weights": jnp.clip(jnp.exp(math.log(0.35) - 0.8472978 * jax.random.uniform(seeds[3], (SUBS, REGIONS, ORDER), jnp.float32) ** block_scale(seeds[3], (SUBS, REGIONS, ORDER), ((0, 8), (1, 4)), -0.2, 0.2)), 0.15, 0.35),
        "face_map": draw_face_map(jax.random.fold_in(seeds[9], 71), 0),
        "matching": jax.vmap(lambda own: jax.random.permutation(own, TILE))(jax.random.split(seeds[5], SUBS * REGIONS * 6)).reshape((SUBS, REGIONS, 6, TILE)).astype(jnp.int32),
        "coarse_basis": scatter_about(seeds[6], (SUBS, REGIONS, ORDER, COARSE), ORDER ** -0.5, 0.15625, ((0, 8), (1, 4))),
        "coarse_map": draw_coarse_map(jax.random.fold_in(seeds[9], 71), 0),
        "coarse_inverse": draw_coarse_inverse(jax.random.fold_in(seeds[9], 71), 0),
    }


def subdomain_products(tiles, tile_list, values):
    total = SUBS * REGIONS
    flat_tiles = tiles.reshape(total, LISTED, TILE, TILE)
    flat_lists = tile_list.reshape(total, LISTED, 2)
    flat_values = values.reshape(total, ORDER, RIGHTS)

    def single(item):
        block, listing, vector = item
        low = lax.optimization_barrier(vector.astype(jnp.bfloat16)).astype(jnp.float32)
        low = low.reshape(BLOCKS, TILE, RIGHTS)
        picked = low[listing[:, 1]]
        products = jnp.einsum("tij,tjr->tir", block.astype(jnp.float32), picked, precision=lax.Precision.HIGHEST)
        table = (listing[:, 0][None, :] == jnp.arange(BLOCKS, dtype=jnp.int32)[:, None]).astype(jnp.float32)
        summed = jnp.einsum("bt,tir->bir", table, products, precision=lax.Precision.HIGHEST)
        return summed.reshape(ORDER, RIGHTS)

    return lax.map(single, (flat_tiles, flat_lists, flat_values)).reshape(SUBS, REGIONS, ORDER, RIGHTS)


def face_coupling(values, face_map, matching):
    stride = max(N_REG // 4, 1)
    stacked = values.reshape(SUBS, REGIONS, BLOCKS, TILE, RIGHTS)
    faces = jnp.take_along_axis(stacked, face_map[:, :, :, None, None], axis=2)
    moves = ((1, 1), (1, -1), (1, stride), (1, -stride), (0, 1), (0, -1))
    coupling = jnp.zeros_like(stacked)
    block_ids = jnp.arange(BLOCKS, dtype=jnp.int32)
    for face in range(6):
        along, offset = moves[face]
        arrived = jnp.roll(faces[:, :, face ^ 1], offset, axis=along)
        permuted = jnp.take_along_axis(arrived, matching[:, :, face, :, None], axis=2)
        table = (face_map[:, :, face][:, :, None] == block_ids[None, None, :]).astype(jnp.float32)
        coupling = coupling + table[:, :, :, None, None] * permuted[:, :, None]
    return coupling.reshape(SUBS, REGIONS, ORDER, RIGHTS)


def operator(values, tiles, tile_list, face_map, matching):
    return subdomain_products(tiles, tile_list, values) - 0.5 * face_coupling(values, face_map, matching)


def precondition(residual, weights, coarse_basis, coarse_map, coarse_inverse):
    basis = coarse_basis.astype(jnp.float32)
    low = lax.optimization_barrier(residual.astype(jnp.bfloat16)).astype(jnp.float32)
    local_coarse = jnp.einsum("sgmn,sgmr->sgnr", basis, low, precision=lax.Precision.HIGHEST)
    region_ids = jnp.broadcast_to(jnp.arange(REGIONS, dtype=jnp.int32)[None, :, None], (SUBS, REGIONS, COARSE))
    assembled = jnp.zeros((REGIONS, COARSE_ALL, RIGHTS), jnp.float32).at[region_ids, coarse_map].add(local_coarse)
    coarse_solution = jnp.einsum("gab,gbr->gar", coarse_inverse, assembled, precision=lax.Precision.HIGHEST)
    own = coarse_solution[region_ids, coarse_map]
    own_low = lax.optimization_barrier(own.astype(jnp.bfloat16)).astype(jnp.float32)
    correction = jnp.einsum("sgmn,sgnr->sgmr", basis, own_low, precision=lax.Precision.HIGHEST)
    return weights[:, :, :, None] * residual + correction


def reference(right_side, tiles, tile_list, weights, face_map, matching, coarse_basis, coarse_map, coarse_inverse):
    solution = jnp.zeros_like(right_side)
    residual = right_side
    for sweep in range(SWEEPS):
        solution = solution + precondition(residual, weights, coarse_basis, coarse_map, coarse_inverse)
        residual = right_side - operator(solution, tiles, tile_list, face_map, matching)
    return solution.astype(jnp.bfloat16), residual.astype(jnp.bfloat16)
```

```python
import functools

import jax
import jax.numpy as jnp
from jax import lax
from jax.experimental import pallas as pl
from jax.experimental.pallas import tpu as pltpu
from jax.sharding import PartitionSpec as P

SWEEPS = 3
F32 = jnp.float32
BF16 = jnp.bfloat16
I32 = jnp.int32
VMEM = pl.BlockSpec(memory_space=pltpu.VMEM)
ANY = pl.BlockSpec(memory_space=pl.ANY)
SMEM = pl.BlockSpec(memory_space=pltpu.SMEM)
NT = (((1,), (1,)), ((), ()))
NN = (((1,), (0,)), ((), ()))


def matmul(a, b, dims):
    return lax.dot_general(a, b, dims, preferred_element_type=F32)


def at_block(block, tile):
    return pl.ds(pl.multiple_of(block * tile, tile), tile)


def lanes(ref):
    return jnp.concatenate([ref[b] for b in range(ref.shape[0])], axis=1)


def one_hot(mask):
    return mask.astype(F32).astype(BF16)


def put_all(ref, value):
    def put(i, carry):
        ref[i] = value
        return carry

    lax.fori_loop(0, ref.shape[0], put, 0, unroll=min(8, ref.shape[0]))


def first_kernel(place_ref, rhs_ref, basis_ref, inverse_ref, ids_ref, chunk_ref):
    rights = rhs_ref.shape[0]
    held, total = inverse_ref.shape
    coarse = matmul(rhs_ref[...].astype(BF16), basis_ref[...], NN)
    ids = ids_ref[...]
    high = (ids // 128).astype(F32)
    low = (ids % 128).astype(F32)
    count = ids.shape[1]
    own_diagonal = lax.broadcasted_iota(I32, (held, total), 1) == (
        lax.broadcasted_iota(I32, (held, total), 0) + place_ref[0] * held
    )
    rows = inverse_ref[...]
    rounded = rows.astype(BF16)
    dropped = jnp.where(own_diagonal, rows - rounded.astype(F32), 0.0)
    dropped = jnp.sum(dropped, axis=0, keepdims=True)
    codes = [high, low] + [dropped[:, q * count : (q + 1) * count] for q in range(total // count)]
    code_rows = -(-len(codes) // 16) * 16
    row = lax.broadcasted_iota(I32, (code_rows, count), 0)
    coded = jnp.zeros((code_rows, count), F32)
    for n, code in enumerate(codes):
        coded = jnp.where(row == n, code, coded)
    pieces = [coded.astype(BF16), coarse.astype(BF16)]
    for q in range(total // count):
        pieces.append(rounded[:, q * count : (q + 1) * count])
    put_all(chunk_ref, jnp.concatenate(pieces, axis=0))


def update(z, basis_ref, weights_ref, u, r, place_ref, faces_ref, new_ref, low_ref, out_refs, groups):
    tile = out_refs[0].shape[2]
    value = weights_ref[...] * r + matmul(z.astype(BF16), basis_ref[...], NT)
    if u is not None:
        value = u + value
    new_ref[...] = value
    low_ref[...] = value.astype(BF16)
    for out_ref, (faces, turn) in zip(out_refs, groups, strict=True):
        for n, face in enumerate(faces):
            out_ref[n] = low_ref[:, at_block(faces_ref[0, face ^ place_ref[turn]], tile)]


def opening_kernel(
    groups,
    total,
    place_ref,
    faces_ref,
    tiles_ref,
    ids_ref,
    got_ref,
    basis_ref,
    weights_ref,
    r_ref,
    kept_ref,
    block_ref,
    new_ref,
    low_ref,
    *refs,
):
    *out_refs, sem = refs
    copy = pltpu.make_async_copy(tiles_ref, kept_ref, sem)
    copy.start()
    peers = got_ref.shape[0]
    rights = r_ref.shape[0]
    count = ids_ref.shape[1]
    parts = total // count
    code_rows = -(-(2 + parts) // 16) * 16
    body_at = code_rows + rights
    held = (got_ref.shape[1] - body_at) // parts
    codes = [got_ref[i, :code_rows, :].astype(F32) for i in range(peers)]
    dropped = sum(codes)
    column = jnp.broadcast_to(ids_ref[...].astype(F32), (count, count)).T
    lane = lax.broadcasted_iota(I32, (count, count), 1).astype(F32)
    own = [column == lane + float(q * count) for q in range(parts)]
    own_low = jnp.concatenate([one_hot(hot) for hot in own], axis=1)
    own_rows, own_dropped = [], []
    for q in range(parts):
        piece = got_ref[:, body_at + q * held : body_at + (q + 1) * held, :].reshape(peers * held, count)
        own_rows.append(matmul(own_low, piece, NN).astype(BF16))
        own_dropped.append(jnp.where(own[q], dropped[2 + q : 3 + q], 0.0).astype(BF16))
    own_rows = jnp.concatenate(
        [jnp.concatenate(own_rows, axis=1), jnp.concatenate(own_dropped, axis=1)], axis=0
    )
    index = lax.broadcasted_iota(I32, (total, count), 0).astype(F32)
    z = jnp.zeros((rights, count), F32)
    for i in range(peers):
        ids = codes[i][0:1] * 128.0 + codes[i][1:2]
        piece = matmul(own_rows, one_hot(index == ids), NN).astype(BF16)
        block_ref[i] = piece
        both = matmul(got_ref[i, code_rows:body_at, :], piece, NT)
        z = z + both[:, :count] + both[:, count:]
    update(z, basis_ref, weights_ref, None, r_ref[...], place_ref, faces_ref, new_ref, low_ref, out_refs, groups)
    copy.wait()


def correct_kernel(
    groups, place_ref, faces_ref, got_ref, block_ref, basis_ref, weights_ref, u_ref, r_ref, new_ref, low_ref, *out_refs
):
    count = got_ref.shape[2]
    both = matmul(lanes(got_ref), lanes(block_ref), NT)
    z = both[:, :count] + both[:, count:]
    update(z, basis_ref, weights_ref, u_ref[...], r_ref[...], place_ref, faces_ref, new_ref, low_ref, out_refs, groups)


def local_kernel(list_ref, x_ref, tiles_ref, y_ref):
    tile = tiles_ref.shape[1]
    for t in range(tiles_ref.shape[0]):
        product = matmul(x_ref[:, at_block(list_ref[1, t], tile)], tiles_ref[t], NT)
        cut = at_block(list_ref[0, t], tile)
        if t * tile < y_ref.shape[1]:
            y_ref[:, t * tile : (t + 1) * tile] = product
        else:
            y_ref[:, cut] = y_ref[:, cut] + product


def couple(groups, place_ref, faces_ref, match_ref, rhs_ref, y_ref, in_refs, r_ref):
    tile = match_ref.shape[2]
    r_ref[...] = rhs_ref[...] - y_ref[...]
    index = lax.broadcasted_iota(I32, (tile, tile), 0)
    for in_ref, (faces, turn) in zip(in_refs, groups, strict=True):
        for n, first in enumerate(faces):
            face = first ^ place_ref[turn]
            got = matmul(in_ref[n], one_hot(index == match_ref[face]), NN)
            cut = at_block(faces_ref[0, face], tile)
            r_ref[:, cut] = r_ref[:, cut] + 0.5 * got


def residual_kernel(groups, place_ref, faces_ref, match_ref, rhs_ref, y_ref, basis_ref, *refs):
    in_refs, (r_ref, chunk_ref) = refs[: len(groups)], refs[len(groups) :]
    couple(groups, place_ref, faces_ref, match_ref, rhs_ref, y_ref, in_refs, r_ref)
    put_all(chunk_ref, matmul(r_ref[...].astype(BF16), basis_ref[...], NN).astype(BF16))


def last_kernel(groups, place_ref, faces_ref, match_ref, rhs_ref, y_ref, *refs):
    in_refs, (out_ref, r_ref) = refs[: len(groups)], refs[len(groups) :]
    couple(groups, place_ref, faces_ref, match_ref, rhs_ref, y_ref, in_refs, r_ref)
    out_ref[...] = r_ref[...].astype(BF16)


def near(*arrays):
    return [pltpu.with_memory_space_constraint(a, pltpu.VMEM) for a in arrays]


def call(kernel, outs, scalars, *args, scratch=(), far=()):
    return pl.pallas_call(
        kernel,
        out_shape=outs,
        in_specs=[SMEM] * len(scalars) + [ANY] * len(far) + [VMEM] * len(args),
        out_specs=[VMEM] * len(outs),
        scratch_shapes=list(scratch),
        compiler_params=pltpu.CompilerParams(vmem_limit_bytes=16 << 20),
    )(*scalars, *far, *args)


def body(
    right_side,
    tiles,
    tile_list,
    weights,
    face_map,
    matching,
    coarse_basis,
    coarse_map,
    coarse_inverse,
):
    order, rights = right_side.shape[2:]
    tile = tiles.shape[3]
    listing = tile_list[0, 0].T
    scaling = weights[0]
    faces_here = face_map[0]
    ids = coarse_map[0]
    count = ids.shape[1]
    inverse_rows = coarse_inverse[0]
    held, total = inverse_rows.shape
    peers = lax.axis_size("sub")
    stride = max(lax.axis_size("reg") // 4, 1)
    place = jnp.stack(
        [lax.axis_index("sub"), lax.axis_index("sub") % 2]
        + [lax.axis_index("reg") // far % 2 for far in sorted({1, stride})]
    ).astype(I32)
    if stride == 1:
        swaps = (((0, 2), "reg", 1, False, 2), ((1, 3), "reg", 1, True, 2))
    else:
        swaps = (
            ((0,), "reg", 1, False, 2),
            ((2,), "reg", stride, False, 3),
            ((1,), "reg", 1, True, 2),
            ((3,), "reg", stride, True, 3),
        )
    swaps = ((((4,), "sub", 1, False, 1),) + swaps + (((5,), "sub", 1, True, 1),))
    groups = tuple((faces, turn) for faces, _, _, _, turn in swaps)

    def swap(shard, axis, far, ahead):
        n = lax.axis_size(axis)
        assert n // far % 2 == 0
        pairs = []
        for i in range(n):
            if (i // far % 2 == 0) == ahead:
                pairs += [(i, (i + far) % n), ((i + far) % n, i)]
        return lax.ppermute(shard, axis, pairs)

    near_out, far_out = pltpu.VMEM, jax.ShapeDtypeStruct
    field = near_out((rights, order), F32)
    field_low = near_out((rights, order), BF16)
    face_outs = [far_out((len(faces), rights, tile), BF16) for faces, _ in groups]
    parts = total // count
    rows = -(-(2 + parts) // 16) * 16 + rights + held * parts

    def spread(chunk):
        return near(lax.all_to_all(chunk, "sub", split_axis=0, concat_axis=0, tiled=True))[0]

    rhs, basis, matched = near(right_side[0, 0].T, coarse_basis[0, 0], matching[0].reshape(-1, 1, tile))
    (chunk,) = call(
        first_kernel, [far_out((peers, rows, count), BF16)], [place], rhs, basis, inverse_rows, ids
    )
    residual = rhs
    got = spread(chunk)
    for sweep in range(SWEEPS):
        if sweep == 0:
            tile_block, block, u, low, *faces = call(
                functools.partial(opening_kernel, groups, total),
                [
                    near_out(tiles.shape[2:], BF16),
                    near_out((peers, 2 * count, count), BF16),
                    field,
                    field_low,
                    *face_outs,
                ],
                [place, faces_here],
                ids,
                got,
                basis,
                scaling,
                residual,
                far=[tiles[0, 0]],
                scratch=[pltpu.SemaphoreType.DMA],
            )
        else:
            u, low, *faces = call(
                functools.partial(correct_kernel, groups),
                [field, field_low, *face_outs],
                [place, faces_here],
                got,
                block,
                basis,
                scaling,
                u,
                residual,
            )
        arrived = near(*[swap(f, *how[1:4]) for f, how in zip(faces, swaps, strict=True)])
        (local,) = call(local_kernel, [field], [listing], low, tile_block)
        if sweep + 1 < SWEEPS:
            residual, chunk = call(
                functools.partial(residual_kernel, groups),
                [field, far_out((peers, rights, count), BF16)],
                [place, faces_here],
                matched,
                rhs,
                local,
                basis,
                *arrived,
            )
            got = spread(chunk)
        else:
            (left,) = call(
                functools.partial(last_kernel, groups),
                [jax.ShapeDtypeStruct((rights, order), BF16)],
                [place, faces_here],
                matched,
                rhs,
                local,
                *arrived,
                scratch=[pltpu.VMEM((rights, order), F32)],
            )
    return low.T[None, None], left.T[None, None]


def solution(mesh):
    placed = (
        P("sub", "reg", None, None),
        P("sub", "reg", None, None, None),
        P("sub", "reg", None, None),
        P("sub", "reg", None),
        P("sub", "reg", None),
        P("sub", "reg", None, None),
        P("sub", "reg", None, None),
        P("sub", "reg", None),
        P("reg", "sub", None),
    )
    return jax.shard_map(
        body,
        mesh=mesh,
        in_specs=placed,
        out_specs=(P("sub", "reg", None, None), P("sub", "reg", None, None)),
        check_vma=False,
    )
```

```python
import functools

import jax
import jax.numpy as jnp
from jax import lax
from jax.experimental import pallas as pl
from jax.experimental.pallas import tpu as pltpu
from jax.sharding import PartitionSpec as P

SWEEPS = 3
F32 = jnp.float32
BF16 = jnp.bfloat16
I32 = jnp.int32
VMEM = pl.BlockSpec(memory_space=pltpu.VMEM)
FAR = pl.BlockSpec(memory_space=pltpu.HBM)
SMEM = pl.BlockSpec(memory_space=pltpu.SMEM)
NT = (((1,), (1,)), ((), ()))
NN = (((1,), (0,)), ((), ()))


def matmul(a, b, dims):
    return lax.dot_general(a, b, dims, preferred_element_type=F32)


def at_block(block, tile):
    return pl.ds(pl.multiple_of(block * tile, tile), tile)


def lanes(ref):
    return jnp.concatenate([ref[b] for b in range(ref.shape[0])], axis=1)


def one_hot(mask):
    return mask.astype(F32).astype(BF16)


def blocks_of(value, tile):
    return [value[:, at : at + tile] for at in range(0, value.shape[1], tile)]


def code_rows(parts):
    return -(-(2 + parts) // 16) * 16


def first_kernel(
    groups,
    place_ref,
    rhs_far,
    basis_far,
    inverse_far,
    weights_far,
    ids_far,
    faces_far,
    chunk_far,
    rhs_ref,
    basis_ref,
    weights_ref,
    ids_ref,
    masks_ref,
    inverse_ref,
    packed_ref,
    faces_ref,
    in_sems,
    out_sems,
):
    pairs = (
        (inverse_far, inverse_ref),
        (ids_far, ids_ref),
        (rhs_far, rhs_ref),
        (basis_far, basis_ref),
        (weights_far, weights_ref),
        (faces_far, faces_ref),
    )
    copies = [pltpu.make_async_copy(*pair, in_sems.at[n]) for n, pair in enumerate(pairs)]
    for copy in copies:
        copy.start()
    rights = rhs_ref.shape[0]
    held, total = inverse_ref.shape
    count = ids_ref.shape[1]
    parts = total // count
    head = code_rows(parts)
    copies[0].wait()
    copies[1].wait()
    ids = ids_ref[...]
    on_diagonal = lax.broadcasted_iota(I32, (held, total), 1) == (
        lax.broadcasted_iota(I32, (held, total), 0) + place_ref[0] * held
    )
    inverse = inverse_ref[...]
    rounded = inverse.astype(BF16)
    dropped = jnp.where(on_diagonal, inverse - rounded.astype(F32), 0.0)
    dropped = jnp.sum(dropped, axis=0, keepdims=True)
    codes = [(ids // 128).astype(F32), (ids % 128).astype(F32)] + blocks_of(dropped, count)
    row = lax.broadcasted_iota(I32, (head, count), 0)
    coded = jnp.zeros((head, count), F32)
    for n, code in enumerate(codes):
        coded = jnp.where(row == n, code, coded)
    packed_ref[:head] = coded.astype(BF16)
    for q, piece in enumerate(blocks_of(rounded, count)):
        at = head + rights + q * held
        packed_ref[at : at + held] = piece
    copies[2].wait()
    copies[3].wait()
    packed_ref[head : head + rights] = matmul(rhs_ref[...].astype(BF16), basis_ref[...], NN).astype(BF16)
    outs = [
        pltpu.make_async_copy(packed_ref, chunk_far.at[i], out_sems.at[i])
        for i in range(chunk_far.shape[0])
    ]
    for copy in outs:
        copy.start()
    copies[4].wait()
    copies[5].wait()
    flat = [(face, turn) for faces, turn in groups for face in faces]
    block = lax.broadcasted_iota(I32, masks_ref.shape[1:], 0)
    for n, (face, turn) in enumerate(flat):
        masks_ref[n] = (block == faces_ref[0, face ^ place_ref[turn]]).astype(F32)
    for copy in outs:
        copy.wait()


def update(z, basis_ref, weights_ref, u, r, masks_ref, new_ref, out_refs):
    tile = out_refs[0].shape[2]
    value = weights_ref[...] * r + matmul(z.astype(BF16), basis_ref[...], NT)
    if u is not None:
        value = u + value
    new_ref[...] = value
    blocks = blocks_of(value, tile)
    at = 0
    for out_ref in out_refs:
        for n in range(out_ref.shape[0]):
            face = sum(masks_ref[at, b : b + 1] * block for b, block in enumerate(blocks))
            out_ref[n] = face.astype(BF16)
            at += 1


def opening_kernel(total, ids_ref, got_ref, basis_ref, weights_ref, r_ref, masks_ref, block_ref, new_ref, *out_refs):
    peers = got_ref.shape[0]
    rights = r_ref.shape[0]
    count = ids_ref.shape[1]
    parts = total // count
    head = code_rows(parts)
    body_at = head + rights
    held = (got_ref.shape[1] - body_at) // parts
    codes = [got_ref[i, :head, :].astype(F32) for i in range(peers)]
    dropped = sum(codes)
    column = jnp.broadcast_to(ids_ref[...].astype(F32), (count, count)).T
    lane = lax.broadcasted_iota(I32, (count, count), 1).astype(F32)
    own = [column == lane + float(q * count) for q in range(parts)]
    own_low = jnp.concatenate([one_hot(hot) for hot in own], axis=1)
    own_rows, own_dropped = [], []
    for q in range(parts):
        piece = got_ref[:, body_at + q * held : body_at + (q + 1) * held, :].reshape(peers * held, count)
        own_rows.append(matmul(own_low, piece, NN).astype(BF16))
        own_dropped.append(jnp.where(own[q], dropped[2 + q : 3 + q], 0.0).astype(BF16))
    own_rows = jnp.concatenate(
        [jnp.concatenate(own_rows, axis=1), jnp.concatenate(own_dropped, axis=1)], axis=0
    )
    index = lax.broadcasted_iota(I32, (total, count), 0).astype(F32)
    z = jnp.zeros((rights, count), F32)
    for i in range(peers):
        ids = codes[i][0:1] * 128.0 + codes[i][1:2]
        piece = matmul(own_rows, one_hot(index == ids), NN).astype(BF16)
        block_ref[i] = piece
        both = matmul(got_ref[i, head:body_at, :], piece, NT)
        z = z + both[:, :count] + both[:, count:]
    update(z, basis_ref, weights_ref, None, r_ref[...], masks_ref, new_ref, out_refs)


def correct_kernel(got_ref, block_ref, basis_ref, weights_ref, u_ref, r_ref, masks_ref, new_ref, *out_refs):
    count = got_ref.shape[2]
    both = matmul(lanes(got_ref), lanes(block_ref), NT)
    z = both[:, :count] + both[:, count:]
    update(z, basis_ref, weights_ref, u_ref[...], r_ref[...], masks_ref, new_ref, out_refs)


def subtract_tile(t, list_ref, low_ref, tile_ref, rhs_ref, base_ref):
    tile = tile_ref.shape[0]
    product = matmul(low_ref[:, at_block(list_ref[1, t], tile)], tile_ref[...], NT)
    if t * tile < base_ref.shape[1]:
        cut = slice(t * tile, (t + 1) * tile)
        base_ref[:, cut] = rhs_ref[:, cut] - product
    else:
        cut = at_block(list_ref[0, t], tile)
        base_ref[:, cut] = base_ref[:, cut] - product


def local_kernel(list_ref, u_ref, tiles_ref, rhs_ref, base_ref, low_ref):
    low_ref[...] = u_ref[...].astype(BF16)
    for t in range(tiles_ref.shape[0]):
        subtract_tile(t, list_ref, low_ref, tiles_ref.at[t], rhs_ref, base_ref)


def local_first_kernel(groups, list_ref, place_ref, u_ref, tiles_ref, rhs_ref, match_ref, base_ref, low_ref, tables_ref):
    flat = [(face, turn) for faces, turn in groups for face in faces]
    index = lax.broadcasted_iota(I32, tables_ref.shape[1:], 0)
    for n, (face, turn) in enumerate(flat):
        tables_ref[n] = one_hot(index == match_ref[face ^ place_ref[turn]])
    local_kernel(list_ref, u_ref, tiles_ref, rhs_ref, base_ref, low_ref)


def coupled(tables_ref, masks_ref, base_ref, in_refs):
    got = []
    for in_ref in in_refs:
        for n in range(in_ref.shape[0]):
            got.append(0.5 * matmul(in_ref[n], tables_ref[len(got)], NN))
    blocks = blocks_of(base_ref[...], got[0].shape[1])
    return jnp.concatenate(
        [
            block + sum(masks_ref[n, b : b + 1] * face for n, face in enumerate(got))
            for b, block in enumerate(blocks)
        ],
        axis=1,
    )


def residual_kernel(tables_ref, masks_ref, base_ref, basis_ref, *refs):
    *in_refs, r_ref, chunk_ref = refs
    residual = coupled(tables_ref, masks_ref, base_ref, in_refs)
    r_ref[...] = residual
    coarse = matmul(residual.astype(BF16), basis_ref[...], NN).astype(BF16)
    for i in range(chunk_ref.shape[0]):
        chunk_ref[i] = coarse


def last_kernel(tables_ref, masks_ref, base_ref, *refs):
    *in_refs, out_ref = refs
    out_ref[...] = coupled(tables_ref, masks_ref, base_ref, in_refs).astype(BF16)


def call(kernel, outs, args, scalars=0, far_args=0, far_outs=0, scratch=()):
    return pl.pallas_call(
        kernel,
        out_shape=outs,
        in_specs=[SMEM] * scalars + [FAR] * far_args + [VMEM] * (len(args) - scalars - far_args),
        out_specs=[FAR] * far_outs + [VMEM] * (len(outs) - far_outs),
        scratch_shapes=list(scratch),
        compiler_params=pltpu.CompilerParams(vmem_limit_bytes=16 << 20),
    )(*args)


def far(array):
    return pltpu.with_memory_space_constraint(array, pltpu.HBM)


def near(array):
    return pltpu.with_memory_space_constraint(array, pltpu.VMEM)


def body(
    right_side,
    tiles,
    tile_list,
    weights,
    face_map,
    matching,
    coarse_basis,
    coarse_map,
    coarse_inverse,
):
    order, rights = right_side.shape[2:]
    tile = tiles.shape[3]
    listing = tile_list[0, 0].T
    count = coarse_map.shape[2]
    inverse_rows = coarse_inverse[0]
    held, total = inverse_rows.shape
    peers = lax.axis_size("sub")
    stride = max(lax.axis_size("reg") // 4, 1)
    place = jnp.stack(
        [lax.axis_index("sub"), lax.axis_index("sub") % 2]
        + [lax.axis_index("reg") // far % 2 for far in sorted({1, stride})]
    ).astype(I32)
    if stride == 1:
        swaps = (((0, 2), "reg", 1, False, 2), ((1, 3), "reg", 1, True, 2))
    else:
        swaps = (
            ((0,), "reg", 1, False, 2),
            ((2,), "reg", stride, False, 3),
            ((1,), "reg", 1, True, 2),
            ((3,), "reg", stride, True, 3),
        )
    swaps = ((((4,), "sub", 1, False, 1),) + swaps + (((5,), "sub", 1, True, 1),))
    groups = tuple((faces, turn) for faces, _, _, _, turn in swaps)

    def swap(shard, axis, far, ahead):
        n = lax.axis_size(axis)
        assert n // far % 2 == 0
        pairs = []
        for i in range(n):
            if (i // far % 2 == 0) == ahead:
                pairs += [(i, (i + far) % n), ((i + far) % n, i)]
        return lax.ppermute(shard, axis, pairs)

    near_out, far_out = pltpu.VMEM, jax.ShapeDtypeStruct
    field = near_out((rights, order), F32)
    face_outs = [far_out((len(faces), rights, tile), BF16) for faces, _ in groups]
    face_count = sum(len(faces) for faces, _ in groups)
    parts = total // count
    rows = code_rows(parts) + rights + held * parts

    def spread(chunk):
        return near(lax.all_to_all(chunk, "sub", split_axis=0, concat_axis=0, tiled=True))

    chunk, rhs, basis, scaling, ids, masks = call(
        functools.partial(first_kernel, groups),
        [
            far_out((peers, rows, count), BF16),
            field,
            near_out((order, count), BF16),
            near_out((1, order), F32),
            near_out((1, count), I32),
            near_out((face_count, -(-(order // tile) // 8) * 8, tile), F32),
        ],
        [
            place,
            far(right_side[0, 0].T),
            far(coarse_basis[0, 0]),
            far(inverse_rows),
            far(weights[0]),
            far(coarse_map[0]),
            far(face_map[0]),
        ],
        scalars=1,
        far_args=6,
        far_outs=1,
        scratch=[
            pltpu.VMEM((held, total), F32),
            pltpu.VMEM((rows, count), BF16),
            pltpu.SMEM(face_map.shape[1:], I32),
            pltpu.SemaphoreType.DMA((6,)),
            pltpu.SemaphoreType.DMA((peers,)),
        ],
    )
    tile_block = tiles[0, 0]
    residual = rhs
    for sweep in range(SWEEPS):
        got = spread(chunk)
        if sweep == 0:
            block, u, *faces = call(
                functools.partial(opening_kernel, total),
                [near_out((peers, 2 * count, count), BF16), field, *face_outs],
                [ids, got, basis, scaling, residual, masks],
            )
        else:
            u, *faces = call(
                correct_kernel, [field, *face_outs], [got, block, basis, scaling, u, residual, masks]
            )
        arrived = [near(swap(face, *how[1:4])) for face, how in zip(faces, swaps, strict=True)]
        low_out = (near_out if sweep + 1 < SWEEPS else far_out)((rights, order), BF16)
        if sweep == 0:
            base, low, tables = call(
                functools.partial(local_first_kernel, groups),
                [field, low_out, near_out((face_count, tile, tile), BF16)],
                [listing, place, u, tile_block, rhs, matching[0].reshape(-1, 1, tile)],
                scalars=2,
            )
        else:
            base, low = call(local_kernel, [field, low_out], [listing, u, tile_block, rhs], scalars=1)
        if sweep + 1 < SWEEPS:
            residual, chunk = call(
                residual_kernel,
                [field, far_out((peers, rights, count), BF16)],
                [tables, masks, base, basis, *arrived],
            )
        else:
            (left,) = call(
                last_kernel, [far_out((rights, order), BF16)], [tables, masks, base, *arrived]
            )
    return low.T[None, None], left.T[None, None]


def solution(mesh):
    placed = (
        P("sub", "reg", None, None),
        P("sub", "reg", None, None, None),
        P("sub", "reg", None, None),
        P("sub", "reg", None),
        P("sub", "reg", None),
        P("sub", "reg", None, None),
        P("sub", "reg", None, None),
        P("sub", "reg", None),
        P("reg", "sub", None),
    )
    return jax.shard_map(
        body,
        mesh=mesh,
        in_specs=placed,
        out_specs=(P("sub", "reg", None, None), P("sub", "reg", None, None)),
        check_vma=False,
    )
```

```python
import functools

import jax
import jax.numpy as jnp
from jax import lax
from jax.experimental import pallas as pl
from jax.experimental.pallas import tpu as pltpu
from jax.sharding import PartitionSpec as P


SWEEPS = 3
F32 = jnp.float32
BF16 = jnp.bfloat16
I32 = jnp.int32
VMEM = pl.BlockSpec(memory_space=pltpu.VMEM)
FAR = pl.BlockSpec(memory_space=pltpu.HBM)
NT = (((1,), (1,)), ((), ()))
NN = (((1,), (0,)), ((), ()))


def matmul(a, b, dims):
    return lax.dot_general(a, b, dims, preferred_element_type=F32)


def at_block(block, tile):
    return pl.ds(pl.multiple_of(block * tile, tile), tile)


def lanes(ref):
    return jnp.concatenate([ref[b] for b in range(ref.shape[0])], axis=1)


def one_hot(mask):
    return mask.astype(F32).astype(BF16)


def blocks_of(value, tile):
    return [value[:, at : at + tile] for at in range(0, value.shape[1], tile)]


def facing(groups):
    return [
        face ^ (lax.axis_index(axis) // apart % 2) for faces, axis, apart in groups for face in faces
    ]


def code_rows(parts):
    return -(-(2 + parts) // 16) * 16


def first_kernel(
    groups,
    rhs_far,
    basis_far,
    inverse_far,
    weights_far,
    ids_far,
    faces_far,
    packed_ref,
    rhs_ref,
    basis_ref,
    weights_ref,
    ids_ref,
    masks_ref,
    inverse_ref,
    faces_ref,
    in_sems,
):
    pairs = (
        (inverse_far, inverse_ref),
        (ids_far, ids_ref),
        (rhs_far, rhs_ref),
        (basis_far, basis_ref),
        (weights_far, weights_ref),
        (faces_far, faces_ref),
    )
    copies = [pltpu.make_async_copy(*pair, in_sems.at[n]) for n, pair in enumerate(pairs)]
    for copy in copies:
        copy.start()
    rights = rhs_ref.shape[0]
    held, total = inverse_ref.shape
    count = ids_ref.shape[1]
    parts = total // count
    head = code_rows(parts)
    copies[0].wait()
    copies[1].wait()
    ids = ids_ref[...]
    on_diagonal = lax.broadcasted_iota(I32, (held, total), 1) == (
        lax.broadcasted_iota(I32, (held, total), 0) + lax.axis_index("sub") * held
    )
    inverse = inverse_ref[...]
    rounded = inverse.astype(BF16)
    dropped = jnp.where(on_diagonal, inverse - rounded.astype(F32), 0.0)
    dropped = jnp.sum(dropped, axis=0, keepdims=True)
    codes = [(ids // 128).astype(F32), (ids % 128).astype(F32)] + blocks_of(dropped, count)
    row = lax.broadcasted_iota(I32, (head, count), 0)
    coded = jnp.zeros((head, count), F32)
    for n, code in enumerate(codes):
        coded = jnp.where(row == n, code, coded)
    packed_ref[:head] = coded.astype(BF16)
    for q, piece in enumerate(blocks_of(rounded, count)):
        at = head + rights + q * held
        packed_ref[at : at + held] = piece
    copies[2].wait()
    copies[3].wait()
    packed_ref[head : head + rights] = matmul(rhs_ref[...].astype(BF16), basis_ref[...], NN).astype(BF16)
    copies[4].wait()
    copies[5].wait()
    block = lax.broadcasted_iota(I32, masks_ref.shape[1:], 0)
    for n, face in enumerate(facing(groups)):
        masks_ref[n] = (block == faces_ref[0, face]).astype(F32)


def update(z, basis_ref, weights_ref, u, r, masks_ref, new_ref, out_refs):
    tile = out_refs[0].shape[2]
    value = weights_ref[...] * r + matmul(z.astype(BF16), basis_ref[...], NT)
    if u is not None:
        value = u + value
    new_ref[...] = value
    blocks = blocks_of(value, tile)
    at = 0
    for out_ref in out_refs:
        for n in range(out_ref.shape[0]):
            face = sum(masks_ref[at, b : b + 1] * block for b, block in enumerate(blocks))
            out_ref[n] = face.astype(BF16)
            at += 1


def opening_kernel(
    total,
    tiles_far,
    match_far,
    ids_ref,
    got_ref,
    basis_ref,
    weights_ref,
    r_ref,
    masks_ref,
    tiles_ref,
    match_ref,
    block_ref,
    new_ref,
    *refs,
):
    *out_refs, sems = refs
    copies = [
        pltpu.make_async_copy(tiles_far, tiles_ref, sems.at[0]),
        pltpu.make_async_copy(match_far, match_ref, sems.at[1]),
    ]
    for copy in copies:
        copy.start()
    peers = got_ref.shape[0]
    rights = r_ref.shape[0]
    count = ids_ref.shape[1]
    parts = total // count
    head = code_rows(parts)
    body_at = head + rights
    held = (got_ref.shape[1] - body_at) // parts
    codes = [got_ref[i, :head, :].astype(F32) for i in range(peers)]
    dropped = sum(codes)
    column = jnp.broadcast_to(ids_ref[...].astype(F32), (count, count)).T
    lane = lax.broadcasted_iota(I32, (count, count), 1).astype(F32)
    own = [column == lane + float(q * count) for q in range(parts)]
    own_low = jnp.concatenate([one_hot(hot) for hot in own], axis=1)
    own_rows, own_dropped = [], []
    for q in range(parts):
        piece = got_ref[:, body_at + q * held : body_at + (q + 1) * held, :].reshape(peers * held, count)
        own_rows.append(matmul(own_low, piece, NN).astype(BF16))
        own_dropped.append(jnp.where(own[q], dropped[2 + q : 3 + q], 0.0).astype(BF16))
    own_rows = jnp.concatenate(
        [jnp.concatenate(own_rows, axis=1), jnp.concatenate(own_dropped, axis=1)], axis=0
    )
    index = lax.broadcasted_iota(I32, (total, count), 0).astype(F32)
    z = jnp.zeros((rights, count), F32)
    for i in range(peers):
        ids = codes[i][0:1] * 128.0 + codes[i][1:2]
        piece = matmul(own_rows, one_hot(index == ids), NN).astype(BF16)
        block_ref[i] = piece
        both = matmul(got_ref[i, head:body_at, :], piece, NT)
        z = z + both[:, :count] + both[:, count:]
    update(z, basis_ref, weights_ref, None, r_ref[...], masks_ref, new_ref, out_refs)
    for copy in copies:
        copy.wait()


def correct_kernel(got_ref, block_ref, basis_ref, weights_ref, u_ref, r_ref, masks_ref, new_ref, *out_refs):
    count = got_ref.shape[2]
    both = matmul(lanes(got_ref), lanes(block_ref), NT)
    z = both[:, :count] + both[:, count:]
    update(z, basis_ref, weights_ref, u_ref[...], r_ref[...], masks_ref, new_ref, out_refs)


def local_kernel(u_ref, rhs_ref, matrix_ref, base_ref, low_ref):
    low = u_ref[...].astype(BF16)
    low_ref[...] = low
    base_ref[...] = rhs_ref[...] - matmul(low, matrix_ref[...], NT)


def local_first_kernel(
    groups, list_far, u_ref, rhs_ref, tiles_ref, match_ref, base_ref, low_ref, tables_ref, matrix_ref, list_ref, sem
):
    tile = tiles_ref.shape[1]
    copy = pltpu.make_async_copy(list_far, list_ref, sem)
    copy.start()
    matrix_ref[...] = jnp.zeros_like(matrix_ref)
    index = lax.broadcasted_iota(I32, tables_ref.shape[1:], 0)
    for n, face in enumerate(facing(groups)):
        tables_ref[n] = one_hot(index == match_ref[face])
    copy.wait()
    for t in range(tiles_ref.shape[0]):
        matrix_ref[at_block(list_ref[0, t], tile), at_block(list_ref[1, t], tile)] = tiles_ref[t]
    local_kernel(u_ref, rhs_ref, matrix_ref, base_ref, low_ref)


def coupled(tables_ref, masks_ref, base_ref, in_refs):
    got = []
    for in_ref in in_refs:
        for n in range(in_ref.shape[0]):
            got.append(0.5 * matmul(in_ref[n], tables_ref[len(got)], NN))
    blocks = blocks_of(base_ref[...], got[0].shape[1])
    return jnp.concatenate(
        [
            block + sum(masks_ref[n, b : b + 1] * face for n, face in enumerate(got))
            for b, block in enumerate(blocks)
        ],
        axis=1,
    )


def residual_kernel(tables_ref, masks_ref, base_ref, basis_ref, *refs):
    *in_refs, r_ref, chunk_ref = refs
    residual = coupled(tables_ref, masks_ref, base_ref, in_refs)
    r_ref[...] = residual
    coarse = matmul(residual.astype(BF16), basis_ref[...], NN).astype(BF16)
    for i in range(chunk_ref.shape[0]):
        chunk_ref[i] = coarse


def last_kernel(tables_ref, masks_ref, base_ref, *refs):
    *in_refs, out_ref = refs
    out_ref[...] = coupled(tables_ref, masks_ref, base_ref, in_refs).astype(BF16)


def call(kernel, outs, args, far_args=0, scratch=()):
    return pl.pallas_call(
        kernel,
        out_shape=outs,
        in_specs=[FAR] * far_args + [VMEM] * (len(args) - far_args),
        out_specs=[VMEM] * len(outs),
        scratch_shapes=list(scratch),
        compiler_params=pltpu.CompilerParams(vmem_limit_bytes=16 << 20),
    )(*args)


def far(array):
    return pltpu.with_memory_space_constraint(array, pltpu.HBM)


def near(array):
    return pltpu.with_memory_space_constraint(array, pltpu.VMEM)


def body(
    right_side,
    tiles,
    tile_list,
    weights,
    face_map,
    matching,
    coarse_basis,
    coarse_map,
    coarse_inverse,
):
    order, rights = right_side.shape[2:]
    tile = tiles.shape[3]
    count = coarse_map.shape[2]
    inverse_rows = coarse_inverse[0]
    held, total = inverse_rows.shape
    peers = lax.axis_size("sub")
    stride = max(lax.axis_size("reg") // 4, 1)
    if stride == 1:
        swaps = (((0, 2), "reg", 1, False), ((1, 3), "reg", 1, True))
    else:
        swaps = (
            ((0,), "reg", 1, False),
            ((2,), "reg", stride, False),
            ((1,), "reg", 1, True),
            ((3,), "reg", stride, True),
        )
    swaps = (((4,), "sub", 1, False),) + swaps + (((5,), "sub", 1, True),)
    groups = tuple(how[:3] for how in swaps)

    def swap(shard, axis, apart, ahead):
        n = lax.axis_size(axis)
        assert n // apart % 2 == 0
        pairs = []
        for i in range(n):
            if (i // apart % 2 == 0) == ahead:
                pairs += [(i, (i + apart) % n), ((i + apart) % n, i)]
        return lax.ppermute(shard, axis, pairs)

    near_out, far_out = pltpu.VMEM, jax.ShapeDtypeStruct
    field = near_out((rights, order), F32)
    face_outs = [far_out((len(faces), rights, tile), BF16) for faces, _, _ in groups]
    face_count = sum(len(faces) for faces, _, _ in groups)
    parts = total // count
    rows = code_rows(parts) + rights + held * parts

    packed, rhs, basis, scaling, ids, masks = call(
        functools.partial(first_kernel, groups),
        [
            far_out((rows, count), BF16),
            field,
            near_out((order, count), BF16),
            near_out((1, order), F32),
            near_out((1, count), I32),
            near_out((face_count, -(-(order // tile) // 8) * 8, tile), F32),
        ],
        [
            far(right_side[0, 0].T),
            far(coarse_basis[0, 0]),
            far(inverse_rows),
            far(weights[0]),
            far(coarse_map[0]),
            far(face_map[0]),
        ],
        far_args=6,
        scratch=[
            pltpu.VMEM((held, total), F32),
            pltpu.SMEM(face_map.shape[1:], I32),
            pltpu.SemaphoreType.DMA((6,)),
        ],
    )
    residual = rhs
    for sweep in range(SWEEPS):
        if sweep == 0:
            got = near(lax.all_gather(packed, "sub", axis=0))
            tile_block, matched, block, u, *faces = call(
                functools.partial(opening_kernel, total),
                [
                    near_out(tiles.shape[2:], BF16),
                    near_out((matching.shape[2], 1, tile), I32),
                    near_out((peers, 2 * count, count), BF16),
                    field,
                    *face_outs,
                ],
                [
                    far(tiles[0, 0]),
                    far(matching[0].reshape(-1, 1, tile)),
                    ids,
                    got,
                    basis,
                    scaling,
                    residual,
                    masks,
                ],
                far_args=2,
                scratch=[pltpu.SemaphoreType.DMA((2,))],
            )
        else:
            got = near(lax.all_to_all(chunk, "sub", split_axis=0, concat_axis=0, tiled=True))
            u, *faces = call(
                correct_kernel, [field, *face_outs], [got, block, basis, scaling, u, residual, masks]
            )
        arrived = []
        for face, how in zip(faces, swaps, strict=True):
            arrived.append(near(swap(face, *how[1:4])))
        low_out = (near_out if sweep + 1 < SWEEPS else far_out)((rights, order), BF16)
        if sweep == 0:
            base, low, tables, matrix = call(
                functools.partial(local_first_kernel, groups),
                [field, low_out, near_out((face_count, tile, tile), BF16), near_out((order, order), BF16)],
                [far(tile_list[0, 0].T), u, rhs, tile_block, matched],
                far_args=1,
                scratch=[pltpu.SMEM(tile_list.shape[:1:-1], I32), pltpu.SemaphoreType.DMA],
            )
        else:
            base, low = call(local_kernel, [field, low_out], [u, rhs, matrix])
        if sweep + 1 < SWEEPS:
            residual, chunk = call(
                residual_kernel,
                [field, far_out((peers, rights, count), BF16)],
                [tables, masks, base, basis, *arrived],
            )
        else:
            (left,) = call(
                last_kernel, [far_out((rights, order), BF16)], [tables, masks, base, *arrived]
            )
    return low.T[None, None], left.T[None, None]


def solution(mesh):
    placed = (
        P("sub", "reg", None, None),
        P("sub", "reg", None, None, None),
        P("sub", "reg", None, None),
        P("sub", "reg", None),
        P("sub", "reg", None),
        P("sub", "reg", None, None),
        P("sub", "reg", None, None),
        P("sub", "reg", None),
        P("reg", "sub", None),
    )
    return jax.shard_map(
        body,
        mesh=mesh,
        in_specs=placed,
        out_specs=(P("sub", "reg", None, None), P("sub", "reg", None, None)),
        check_vma=False,
    )
```

```python
import functools

import jax
import jax.numpy as jnp
from jax import lax
from jax.experimental import pallas as pl
from jax.experimental.pallas import tpu as pltpu
from jax.sharding import PartitionSpec as P


SWEEPS = 3
FETCH = 10
F32 = jnp.float32
BF16 = jnp.bfloat16
I32 = jnp.int32
VMEM = pl.BlockSpec(memory_space=pltpu.VMEM)
FAR = pl.BlockSpec(memory_space=pltpu.HBM)
NT = (((1,), (1,)), ((), ()))
NN = (((1,), (0,)), ((), ()))


def matmul(a, b, dims):
    return lax.dot_general(a, b, dims, preferred_element_type=F32)


def at_block(block, tile):
    return pl.ds(pl.multiple_of(block * tile, tile), tile)


def lanes(ref):
    return jnp.concatenate([ref[b] for b in range(ref.shape[0])], axis=1)


def one_hot(mask):
    return mask.astype(F32).astype(BF16)


def blocks_of(value, tile):
    return [value[:, at : at + tile] for at in range(0, value.shape[1], tile)]


def facing(groups):
    return [
        face ^ (lax.axis_index(axis) // apart % 2) for faces, axis, apart in groups for face in faces
    ]


def inverse_columns(got_ref, at, parts, q):
    peers, rows, count = got_ref.shape
    held = (rows - at) // parts
    return got_ref[:, at + q * held : at + (q + 1) * held, :].reshape(peers * held, count)


def code_rows(parts):
    return -(-(2 + parts) // 16) * 16


def first_kernel(
    groups,
    rhs_far,
    basis_far,
    inverse_far,
    weights_far,
    ids_far,
    faces_far,
    packed_ref,
    rhs_ref,
    basis_ref,
    weights_ref,
    ids_ref,
    masks_ref,
    inverse_ref,
    faces_ref,
    in_sems,
):
    pairs = (
        (inverse_far, inverse_ref),
        (ids_far, ids_ref),
        (rhs_far, rhs_ref),
        (basis_far, basis_ref),
        (weights_far, weights_ref),
        (faces_far, faces_ref),
    )
    copies = [pltpu.make_async_copy(*pair, in_sems.at[n]) for n, pair in enumerate(pairs)]
    for copy in copies:
        copy.start()
    rights = rhs_ref.shape[0]
    held, total = inverse_ref.shape
    count = ids_ref.shape[1]
    parts = total // count
    head = code_rows(parts)
    copies[0].wait()
    copies[1].wait()
    ids = ids_ref[...]
    on_diagonal = lax.broadcasted_iota(I32, (held, total), 1) == (
        lax.broadcasted_iota(I32, (held, total), 0) + lax.axis_index("sub") * held
    )
    inverse = inverse_ref[...]
    rounded = inverse.astype(BF16)
    dropped = jnp.where(on_diagonal, inverse - rounded.astype(F32), 0.0)
    dropped = jnp.sum(dropped, axis=0, keepdims=True)
    codes = [(ids // 128).astype(F32), (ids % 128).astype(F32)] + blocks_of(dropped, count)
    row = lax.broadcasted_iota(I32, (head, count), 0)
    coded = jnp.zeros((head, count), F32)
    for n, code in enumerate(codes):
        coded = jnp.where(row == n, code, coded)
    packed_ref[:head] = coded.astype(BF16)
    for q, piece in enumerate(blocks_of(rounded, count)):
        at = head + rights + q * held
        packed_ref[at : at + held] = piece
    copies[2].wait()
    copies[3].wait()
    packed_ref[head : head + rights] = matmul(rhs_ref[...].astype(BF16), basis_ref[...], NN).astype(BF16)
    copies[4].wait()
    copies[5].wait()
    block = lax.broadcasted_iota(I32, masks_ref.shape[1:], 0)
    for n, face in enumerate(facing(groups)):
        masks_ref[n] = (block == faces_ref[0, face]).astype(F32)


def update(z, basis_ref, weights_ref, u, r, masks_ref, new_ref, out_refs):
    tile = out_refs[0].shape[2]
    value = weights_ref[...] * r + matmul(z.astype(BF16), basis_ref[...], NT)
    if u is not None:
        value = u + value
    new_ref[...] = value
    blocks = blocks_of(value, tile)
    at = 0
    for out_ref in out_refs:
        for n in range(out_ref.shape[0]):
            face = sum(masks_ref[at, b : b + 1] * block for b, block in enumerate(blocks))
            out_ref[n] = face.astype(BF16)
            at += 1


def opening_kernel(
    total,
    tiles_far,
    match_far,
    ids_ref,
    got_ref,
    basis_ref,
    weights_ref,
    r_ref,
    masks_ref,
    matrix_ref,
    tiles_ref,
    match_ref,
    where_ref,
    own_ref,
    new_ref,
    *refs,
):
    *out_refs, sems = refs
    copies = [
        pltpu.make_async_copy(match_far, match_ref, sems.at[0]),
        pltpu.make_async_copy(tiles_far.at[pl.ds(0, tiles_ref.shape[0])], tiles_ref, sems.at[1]),
    ]
    for copy in copies:
        copy.start()
    matrix_ref[...] = jnp.zeros_like(matrix_ref)
    peers = got_ref.shape[0]
    rights = r_ref.shape[0]
    count = ids_ref.shape[1]
    parts = total // count
    head = code_rows(parts)
    codes = [got_ref[i, :head, :].astype(F32) for i in range(peers)]
    index = lax.broadcasted_iota(I32, (total, count), 0).astype(F32)
    for i in range(peers):
        ids = codes[i][0:1] * 128.0 + codes[i][1:2]
        where_ref[:, i * count : (i + 1) * count] = one_hot(index == ids)
    column = jnp.broadcast_to(ids_ref[...].astype(F32), (count, count)).T
    lane = lax.broadcasted_iota(I32, (count, count), 1).astype(F32)
    for q in range(parts):
        own_ref[:, q * count : (q + 1) * count] = one_hot(column == lane + float(q * count))
    coarse = jnp.concatenate([got_ref[i, head : head + rights, :] for i in range(peers)], axis=1)
    assembled = matmul(coarse, where_ref[...], NT)
    high = assembled.astype(BF16)
    both = jnp.concatenate([high, (assembled - high.astype(F32)).astype(BF16)], axis=0)
    dropped = sum(codes)
    z = []
    for q, part in enumerate(blocks_of(assembled, count)):
        product = matmul(both, inverse_columns(got_ref, head + rights, parts, q), NN)
        z.append(product[:rights] + product[rights:] + dropped[2 + q : 3 + q] * part)
    z = jnp.concatenate(z, axis=1).astype(BF16)
    z_own = matmul(z, own_ref[...], NT)
    update(z_own, basis_ref, weights_ref, None, r_ref[...], masks_ref, new_ref, out_refs)
    for copy in copies:
        copy.wait()


def correct_kernel(got_ref, block_ref, basis_ref, weights_ref, u_ref, r_ref, masks_ref, new_ref, *out_refs):
    count = got_ref.shape[2]
    both = matmul(lanes(got_ref), block_ref[...], NT)
    z = both[:, :count] + both[:, count:]
    update(z, basis_ref, weights_ref, u_ref[...], r_ref[...], masks_ref, new_ref, out_refs)


def local_kernel(u_ref, rhs_ref, matrix_ref, base_ref, low_ref):
    low = u_ref[...].astype(BF16)
    low_ref[...] = low
    base_ref[...] = rhs_ref[...] - matmul(low, matrix_ref[...], NT)


def local_first_kernel(
    groups,
    total,
    tiles_far,
    list_far,
    u_ref,
    rhs_ref,
    empty_ref,
    tiles_ref,
    match_ref,
    got_ref,
    where_ref,
    own_ref,
    base_ref,
    low_ref,
    tables_ref,
    block_ref,
    matrix_ref,
    list_ref,
    rest_ref,
    sems,
):
    first, rest = tiles_ref.shape[0], rest_ref.shape[0]
    copies = [
        pltpu.make_async_copy(list_far, list_ref, sems.at[0]),
        pltpu.make_async_copy(tiles_far.at[pl.ds(first, rest)], rest_ref, sems.at[1]),
    ]
    for copy in copies:
        copy.start()
    index = lax.broadcasted_iota(I32, tables_ref.shape[1:], 0)
    for n, face in enumerate(facing(groups)):
        tables_ref[n] = one_hot(index == match_ref[face])
    peers, _, count = got_ref.shape
    parts = total // count
    head = code_rows(parts)
    own = own_ref[...]
    dropped = sum(got_ref[i, :head, :].astype(F32) for i in range(peers))
    own_rows, own_dropped = [], []
    for q in range(parts):
        piece = inverse_columns(got_ref, head + rhs_ref.shape[0], parts, q)
        own_rows.append(matmul(own, piece, NN).astype(BF16))
        own_dropped.append(own[:, q * count : (q + 1) * count] * dropped[2 + q : 3 + q].astype(BF16))
    rows = jnp.concatenate(
        [jnp.concatenate(own_rows, axis=1), jnp.concatenate(own_dropped, axis=1)], axis=0
    )
    block_ref[...] = matmul(rows, where_ref[...], NN).astype(BF16)
    tile = tiles_ref.shape[1]
    copies[0].wait()
    for t in range(first):
        matrix_ref[at_block(list_ref[0, t], tile), at_block(list_ref[1, t], tile)] = tiles_ref[t]
    copies[1].wait()
    for t in range(rest):
        at = at_block(list_ref[0, first + t], tile), at_block(list_ref[1, first + t], tile)
        matrix_ref[at] = rest_ref[t]
    local_kernel(u_ref, rhs_ref, matrix_ref, base_ref, low_ref)


def coupled(tables_ref, masks_ref, base_ref, in_refs):
    got = []
    for in_ref in in_refs:
        for n in range(in_ref.shape[0]):
            got.append(0.5 * matmul(in_ref[n], tables_ref[len(got)], NN))
    blocks = blocks_of(base_ref[...], got[0].shape[1])
    return jnp.concatenate(
        [
            block + sum(masks_ref[n, b : b + 1] * face for n, face in enumerate(got))
            for b, block in enumerate(blocks)
        ],
        axis=1,
    )


def residual_kernel(tables_ref, masks_ref, base_ref, basis_ref, *refs):
    *in_refs, r_ref, chunk_ref = refs
    residual = coupled(tables_ref, masks_ref, base_ref, in_refs)
    r_ref[...] = residual
    coarse = matmul(residual.astype(BF16), basis_ref[...], NN).astype(BF16)
    for i in range(chunk_ref.shape[0]):
        chunk_ref[i] = coarse


def last_kernel(tables_ref, masks_ref, base_ref, *refs):
    *in_refs, out_ref = refs
    out_ref[...] = coupled(tables_ref, masks_ref, base_ref, in_refs).astype(BF16)


def call(kernel, outs, args, far_args=0, scratch=(), aliases=None):
    return pl.pallas_call(
        kernel,
        out_shape=outs,
        in_specs=[FAR] * far_args + [VMEM] * (len(args) - far_args),
        out_specs=[VMEM] * len(outs),
        scratch_shapes=list(scratch),
        input_output_aliases=aliases or {},
        compiler_params=pltpu.CompilerParams(vmem_limit_bytes=16 << 20),
    )(*args)


def far(array):
    return pltpu.with_memory_space_constraint(array, pltpu.HBM)


def near(array):
    return pltpu.with_memory_space_constraint(array, pltpu.VMEM)


def body(
    right_side,
    tiles,
    tile_list,
    weights,
    face_map,
    matching,
    coarse_basis,
    coarse_map,
    coarse_inverse,
):
    order, rights = right_side.shape[2:]
    tile = tiles.shape[3]
    count = coarse_map.shape[2]
    inverse_rows = coarse_inverse[0]
    held, total = inverse_rows.shape
    peers = lax.axis_size("sub")
    stride = max(lax.axis_size("reg") // 4, 1)
    if stride == 1:
        swaps = (((0, 2), "reg", 1, False), ((1, 3), "reg", 1, True))
    else:
        swaps = (
            ((0,), "reg", 1, False),
            ((2,), "reg", stride, False),
            ((1,), "reg", 1, True),
            ((3,), "reg", stride, True),
        )
    swaps = (((4,), "sub", 1, False),) + swaps + (((5,), "sub", 1, True),)
    groups = tuple(how[:3] for how in swaps)

    def swap(shard, axis, apart, ahead):
        n = lax.axis_size(axis)
        assert n // apart % 2 == 0
        pairs = []
        for i in range(n):
            if (i // apart % 2 == 0) == ahead:
                pairs += [(i, (i + apart) % n), ((i + apart) % n, i)]
        return lax.ppermute(shard, axis, pairs)

    near_out, far_out = pltpu.VMEM, jax.ShapeDtypeStruct
    field = near_out((rights, order), F32)
    face_outs = [far_out((len(faces), rights, tile), BF16) for faces, _, _ in groups]
    face_count = sum(len(faces) for faces, _, _ in groups)
    listed = tiles.shape[2]
    fetch = listed * FETCH // 16
    parts = total // count
    rows = code_rows(parts) + rights + held * parts

    packed, rhs, basis, scaling, ids, masks = call(
        functools.partial(first_kernel, groups),
        [
            far_out((rows, count), BF16),
            field,
            near_out((order, count), BF16),
            near_out((1, order), F32),
            near_out((1, count), I32),
            near_out((face_count, -(-(order // tile) // 8) * 8, tile), F32),
        ],
        [
            far(right_side[0, 0].T),
            far(coarse_basis[0, 0]),
            far(inverse_rows),
            far(weights[0]),
            far(coarse_map[0]),
            far(face_map[0]),
        ],
        far_args=6,
        scratch=[
            pltpu.VMEM((held, total), F32),
            pltpu.SMEM(face_map.shape[1:], I32),
            pltpu.SemaphoreType.DMA((6,)),
        ],
    )
    residual = rhs
    for sweep in range(SWEEPS):
        if sweep == 0:
            got = near(lax.all_gather(packed, "sub", axis=0))
            matrix, fetched, matched, where, own, u, *faces = call(
                functools.partial(opening_kernel, total),
                [
                    near_out((order, order), BF16),
                    near_out((fetch, tile, tile), BF16),
                    near_out((matching.shape[2], 1, tile), I32),
                    near_out((total, peers * count), BF16),
                    near_out((count, total), BF16),
                    field,
                    *face_outs,
                ],
                [
                    far(tiles[0, 0]),
                    far(matching[0].reshape(-1, 1, tile)),
                    ids,
                    got,
                    basis,
                    scaling,
                    residual,
                    masks,
                ],
                far_args=2,
                scratch=[pltpu.SemaphoreType.DMA((2,))],
            )
        else:
            got = near(lax.all_to_all(chunk, "sub", split_axis=0, concat_axis=0, tiled=True))
            u, *faces = call(
                correct_kernel, [field, *face_outs], [got, block, basis, scaling, u, residual, masks]
            )
        arrived = []
        for face, how in zip(faces, swaps, strict=True):
            arrived.append(near(swap(face, *how[1:4])))
        low_out = (near_out if sweep + 1 < SWEEPS else far_out)((rights, order), BF16)
        if sweep == 0:
            base, low, tables, block, matrix = call(
                functools.partial(local_first_kernel, groups, total),
                [
                    field,
                    low_out,
                    near_out((face_count, tile, tile), BF16),
                    near_out((2 * count, peers * count), BF16),
                    near_out((order, order), BF16),
                ],
                [far(tiles[0, 0]), far(tile_list[0, 0].T), u, rhs, matrix, fetched, matched, got, where, own],
                far_args=2,
                scratch=[
                    pltpu.SMEM(tile_list.shape[:1:-1], I32),
                    pltpu.VMEM((listed - fetch, tile, tile), BF16),
                    pltpu.SemaphoreType.DMA((2,)),
                ],
                aliases={4: 4},
            )
        else:
            base, low = call(local_kernel, [field, low_out], [u, rhs, matrix])
        if sweep + 1 < SWEEPS:
            residual, chunk = call(
                residual_kernel,
                [field, far_out((peers, rights, count), BF16)],
                [tables, masks, base, basis, *arrived],
            )
        else:
            (left,) = call(
                last_kernel, [far_out((rights, order), BF16)], [tables, masks, base, *arrived]
            )
    return low.T[None, None], left.T[None, None]


def solution(mesh):
    placed = (
        P("sub", "reg", None, None),
        P("sub", "reg", None, None, None),
        P("sub", "reg", None, None),
        P("sub", "reg", None),
        P("sub", "reg", None),
        P("sub", "reg", None, None),
        P("sub", "reg", None, None),
        P("sub", "reg", None),
        P("reg", "sub", None),
    )
    return jax.shard_map(
        body,
        mesh=mesh,
        in_specs=placed,
        out_specs=(P("sub", "reg", None, None), P("sub", "reg", None, None)),
        check_vma=False,
    )
```

```python
import functools

import jax
import jax.numpy as jnp
from jax import lax
from jax.experimental import pallas as pl
from jax.experimental.pallas import tpu as pltpu
from jax.sharding import PartitionSpec as P


SWEEPS = 3
BYTES = 16 << 20
F32 = jnp.float32
BF16 = jnp.bfloat16
I32 = jnp.int32
VMEM = pl.BlockSpec(memory_space=pltpu.VMEM)
FAR = pl.BlockSpec(memory_space=pltpu.HBM)
NT = (((1,), (1,)), ((), ()))
NN = (((1,), (0,)), ((), ()))


def matmul(a, b, dims):
    return lax.dot_general(a, b, dims, preferred_element_type=F32)


def at_block(block, tile):
    return pl.ds(pl.multiple_of(block * tile, tile), tile)


def lanes(ref):
    return jnp.concatenate([ref[b] for b in range(ref.shape[0])], axis=1)


def one_hot(mask):
    return mask.astype(F32).astype(BF16)


def blocks_of(value, tile):
    return [value[:, at : at + tile] for at in range(0, value.shape[1], tile)]


def facing(groups):
    return [
        face ^ (lax.axis_index(axis) // apart % 2) for faces, axis, apart in groups for face in faces
    ]


def inverse_columns(got_ref, at, parts, q):
    peers, rows, count = got_ref.shape
    held = (rows - at) // parts
    return got_ref[:, at + q * held : at + (q + 1) * held, :].reshape(peers * held, count)


def code_rows(parts):
    return -(-(2 + parts) // 16) * 16


def first_kernel(
    groups,
    rhs_far,
    basis_far,
    inverse_far,
    weights_far,
    ids_far,
    faces_far,
    packed_ref,
    rhs_ref,
    basis_ref,
    weights_ref,
    ids_ref,
    masks_ref,
    inverse_ref,
    faces_ref,
    in_sems,
):
    pairs = (
        (inverse_far, inverse_ref),
        (ids_far, ids_ref),
        (rhs_far, rhs_ref),
        (basis_far, basis_ref),
        (weights_far, weights_ref),
        (faces_far, faces_ref),
    )
    copies = [pltpu.make_async_copy(*pair, in_sems.at[n]) for n, pair in enumerate(pairs)]
    for copy in copies:
        copy.start()
    rights = rhs_ref.shape[0]
    held, total = inverse_ref.shape
    count = ids_ref.shape[1]
    parts = total // count
    head = code_rows(parts)
    copies[0].wait()
    copies[1].wait()
    ids = ids_ref[...]
    on_diagonal = lax.broadcasted_iota(I32, (held, total), 1) == (
        lax.broadcasted_iota(I32, (held, total), 0) + lax.axis_index("sub") * held
    )
    inverse = inverse_ref[...]
    rounded = inverse.astype(BF16)
    dropped = jnp.where(on_diagonal, inverse - rounded.astype(F32), 0.0)
    dropped = jnp.sum(dropped, axis=0, keepdims=True)
    codes = [(ids // 128).astype(F32), (ids % 128).astype(F32)] + blocks_of(dropped, count)
    row = lax.broadcasted_iota(I32, (head, count), 0)
    coded = jnp.zeros((head, count), F32)
    for n, code in enumerate(codes):
        coded = jnp.where(row == n, code, coded)
    packed_ref[:head] = coded.astype(BF16)
    for q, piece in enumerate(blocks_of(rounded, count)):
        at = head + rights + q * held
        packed_ref[at : at + held] = piece
    copies[2].wait()
    copies[3].wait()
    packed_ref[head : head + rights] = matmul(rhs_ref[...].astype(BF16), basis_ref[...], NN).astype(BF16)
    copies[4].wait()
    copies[5].wait()
    block = lax.broadcasted_iota(I32, masks_ref.shape[1:], 0)
    for n, face in enumerate(facing(groups)):
        masks_ref[n] = (block == faces_ref[0, face]).astype(F32)


def update(z, basis_ref, weights_ref, u, r, masks_ref, new_ref, out_refs):
    tile = out_refs[0].shape[2]
    value = weights_ref[...] * r + matmul(z.astype(BF16), basis_ref[...], NT)
    if u is not None:
        value = u + value
    new_ref[...] = value
    blocks = blocks_of(value, tile)
    at = 0
    for out_ref in out_refs:
        for n in range(out_ref.shape[0]):
            face = sum(masks_ref[at, b : b + 1] * block for b, block in enumerate(blocks))
            out_ref[n] = face.astype(BF16)
            at += 1


def opening_kernel(
    total,
    match_far,
    ids_ref,
    got_ref,
    basis_ref,
    weights_ref,
    r_ref,
    masks_ref,
    matrix_ref,
    match_ref,
    where_ref,
    own_ref,
    new_ref,
    *refs,
):
    *out_refs, sems = refs
    copies = [pltpu.make_async_copy(match_far, match_ref, sems.at[0])]
    for copy in copies:
        copy.start()
    matrix_ref[...] = jnp.zeros_like(matrix_ref)
    peers = got_ref.shape[0]
    rights = r_ref.shape[0]
    count = ids_ref.shape[1]
    parts = total // count
    head = code_rows(parts)
    codes = [got_ref[i, :head, :].astype(F32) for i in range(peers)]
    index = lax.broadcasted_iota(I32, (total, count), 0).astype(F32)
    for i in range(peers):
        ids = codes[i][0:1] * 128.0 + codes[i][1:2]
        where_ref[:, i * count : (i + 1) * count] = one_hot(index == ids)
    column = jnp.broadcast_to(ids_ref[...].astype(F32), (count, count)).T
    lane = lax.broadcasted_iota(I32, (count, count), 1).astype(F32)
    for q in range(parts):
        own_ref[:, q * count : (q + 1) * count] = one_hot(column == lane + float(q * count))
    coarse = jnp.concatenate([got_ref[i, head : head + rights, :] for i in range(peers)], axis=1)
    assembled = matmul(coarse, where_ref[...], NT)
    high = assembled.astype(BF16)
    both = jnp.concatenate([high, (assembled - high.astype(F32)).astype(BF16)], axis=0)
    dropped = sum(codes)
    z = []
    for q, part in enumerate(blocks_of(assembled, count)):
        product = matmul(both, inverse_columns(got_ref, head + rights, parts, q), NN)
        z.append(product[:rights] + product[rights:] + dropped[2 + q : 3 + q] * part)
    z = jnp.concatenate(z, axis=1).astype(BF16)
    z_own = matmul(z, own_ref[...], NT)
    update(z_own, basis_ref, weights_ref, None, r_ref[...], masks_ref, new_ref, out_refs)
    for copy in copies:
        copy.wait()


def correct_kernel(got_ref, block_ref, basis_ref, weights_ref, u_ref, r_ref, masks_ref, new_ref, *out_refs):
    count = got_ref.shape[2]
    both = matmul(lanes(got_ref), block_ref[...], NT)
    z = both[:, :count] + both[:, count:]
    update(z, basis_ref, weights_ref, u_ref[...], r_ref[...], masks_ref, new_ref, out_refs)


def local_kernel(u_ref, rhs_ref, matrix_ref, base_ref, low_ref):
    low = u_ref[...].astype(BF16)
    low_ref[...] = low
    base_ref[...] = rhs_ref[...] - matmul(low, matrix_ref[...], NT)


def local_first_kernel(
    groups,
    total,
    list_far,
    u_ref,
    rhs_ref,
    empty_ref,
    tiles_ref,
    match_ref,
    got_ref,
    where_ref,
    own_ref,
    base_ref,
    low_ref,
    tables_ref,
    block_ref,
    matrix_ref,
    list_ref,
    sems,
):
    copies = [pltpu.make_async_copy(list_far, list_ref, sems.at[0])]
    copies[0].start()
    index = lax.broadcasted_iota(I32, tables_ref.shape[1:], 0)
    for n, face in enumerate(facing(groups)):
        tables_ref[n] = one_hot(index == match_ref[face])
    peers, _, count = got_ref.shape
    parts = total // count
    head = code_rows(parts)
    own = own_ref[...]
    dropped = sum(got_ref[i, :head, :].astype(F32) for i in range(peers))
    own_rows, own_dropped = [], []
    for q in range(parts):
        piece = inverse_columns(got_ref, head + rhs_ref.shape[0], parts, q)
        own_rows.append(matmul(own, piece, NN).astype(BF16))
        own_dropped.append(own[:, q * count : (q + 1) * count] * dropped[2 + q : 3 + q].astype(BF16))
    rows = jnp.concatenate(
        [jnp.concatenate(own_rows, axis=1), jnp.concatenate(own_dropped, axis=1)], axis=0
    )
    block_ref[...] = matmul(rows, where_ref[...], NN).astype(BF16)
    tile = tiles_ref.shape[1]
    copies[0].wait()
    for t in range(tiles_ref.shape[0]):
        matrix_ref[at_block(list_ref[0, t], tile), at_block(list_ref[1, t], tile)] = tiles_ref[t]
    local_kernel(u_ref, rhs_ref, matrix_ref, base_ref, low_ref)


def coupled(tables_ref, masks_ref, base_ref, in_refs):
    got = []
    for in_ref in in_refs:
        for n in range(in_ref.shape[0]):
            got.append(0.5 * matmul(in_ref[n], tables_ref[len(got)], NN))
    blocks = blocks_of(base_ref[...], got[0].shape[1])
    return jnp.concatenate(
        [
            block + sum(masks_ref[n, b : b + 1] * face for n, face in enumerate(got))
            for b, block in enumerate(blocks)
        ],
        axis=1,
    )


def residual_kernel(tables_ref, masks_ref, base_ref, basis_ref, *refs):
    *in_refs, r_ref, chunk_ref = refs
    residual = coupled(tables_ref, masks_ref, base_ref, in_refs)
    r_ref[...] = residual
    coarse = matmul(residual.astype(BF16), basis_ref[...], NN).astype(BF16)
    for i in range(chunk_ref.shape[0]):
        chunk_ref[i] = coarse


def last_kernel(tables_ref, masks_ref, base_ref, *refs):
    *in_refs, out_ref = refs
    out_ref[...] = coupled(tables_ref, masks_ref, base_ref, in_refs).astype(BF16)


def call(kernel, outs, args, far_args=0, scratch=(), aliases=None, cost=None):
    return pl.pallas_call(
        kernel,
        out_shape=outs,
        in_specs=[FAR] * far_args + [VMEM] * (len(args) - far_args),
        out_specs=[VMEM] * len(outs),
        scratch_shapes=list(scratch),
        input_output_aliases=aliases or {},
        cost_estimate=cost,
        compiler_params=pltpu.CompilerParams(vmem_limit_bytes=16 << 20),
    )(*args)


def far(array):
    return pltpu.with_memory_space_constraint(array, pltpu.HBM)


def near(array):
    return pltpu.with_memory_space_constraint(array, pltpu.VMEM)


def body(
    right_side,
    tiles,
    tile_list,
    weights,
    face_map,
    matching,
    coarse_basis,
    coarse_map,
    coarse_inverse,
):
    order, rights = right_side.shape[2:]
    tile = tiles.shape[3]
    count = coarse_map.shape[2]
    inverse_rows = coarse_inverse[0]
    held, total = inverse_rows.shape
    peers = lax.axis_size("sub")
    stride = max(lax.axis_size("reg") // 4, 1)
    if stride == 1:
        swaps = (((0, 2), "reg", 1, False), ((1, 3), "reg", 1, True))
    else:
        swaps = (
            ((0,), "reg", 1, False),
            ((2,), "reg", stride, False),
            ((1,), "reg", 1, True),
            ((3,), "reg", stride, True),
        )
    swaps = (((4,), "sub", 1, False),) + swaps + (((5,), "sub", 1, True),)
    groups = tuple(how[:3] for how in swaps)

    def swap(shard, axis, apart, ahead):
        n = lax.axis_size(axis)
        assert n // apart % 2 == 0
        pairs = []
        for i in range(n):
            if (i // apart % 2 == 0) == ahead:
                pairs += [(i, (i + apart) % n), ((i + apart) % n, i)]
        return lax.ppermute(shard, axis, pairs)

    near_out, far_out = pltpu.VMEM, jax.ShapeDtypeStruct
    field = near_out((rights, order), F32)
    face_outs = [far_out((len(faces), rights, tile), BF16) for faces, _, _ in groups]
    face_count = sum(len(faces) for faces, _, _ in groups)
    parts = total // count
    rows = code_rows(parts) + rights + held * parts

    packed, rhs, basis, scaling, ids, masks = call(
        functools.partial(first_kernel, groups),
        [
            far_out((rows, count), BF16),
            field,
            near_out((order, count), BF16),
            near_out((1, order), F32),
            near_out((1, count), I32),
            near_out((face_count, -(-(order // tile) // 8) * 8, tile), F32),
        ],
        [
            far(right_side[0, 0].T),
            far(coarse_basis[0, 0]),
            far(inverse_rows),
            far(weights[0]),
            far(coarse_map[0]),
            far(face_map[0]),
        ],
        far_args=6,
        scratch=[
            pltpu.VMEM((held, total), F32),
            pltpu.SMEM(face_map.shape[1:], I32),
            pltpu.SemaphoreType.DMA((6,)),
        ],
    )
    tiles_near = tiles[0, 0]
    residual = rhs
    for sweep in range(SWEEPS):
        if sweep == 0:
            got = near(lax.all_gather(packed, "sub", axis=0))
            matrix, matched, where, own, u, *faces = call(
                functools.partial(opening_kernel, total),
                [
                    near_out((order, order), BF16),
                    near_out((matching.shape[2], 1, tile), I32),
                    near_out((total, peers * count), BF16),
                    near_out((count, total), BF16),
                    field,
                    *face_outs,
                ],
                [
                    far(matching[0].reshape(-1, 1, tile)),
                    ids,
                    got,
                    basis,
                    scaling,
                    residual,
                    masks,
                ],
                far_args=1,
                scratch=[pltpu.SemaphoreType.DMA((1,))],
                cost=pl.CostEstimate(flops=4 * order * order * count, bytes_accessed=BYTES, transcendentals=0),
            )
        else:
            got = near(lax.all_to_all(chunk, "sub", split_axis=0, concat_axis=0, tiled=True))
            u, *faces = call(
                correct_kernel, [field, *face_outs], [got, block, basis, scaling, u, residual, masks]
            )
        arrived = []
        for face, how in zip(faces, swaps, strict=True):
            arrived.append(near(swap(face, *how[1:4])))
        low_out = (near_out if sweep + 1 < SWEEPS else far_out)((rights, order), BF16)
        if sweep == 0:
            base, low, tables, block, matrix = call(
                functools.partial(local_first_kernel, groups, total),
                [
                    field,
                    low_out,
                    near_out((face_count, tile, tile), BF16),
                    near_out((2 * count, peers * count), BF16),
                    near_out((order, order), BF16),
                ],
                [far(tile_list[0, 0].T), u, rhs, matrix, tiles_near, matched, got, where, own],
                far_args=1,
                scratch=[pltpu.SMEM(tile_list.shape[:1:-1], I32), pltpu.SemaphoreType.DMA((1,))],
                aliases={3: 4},
            )
        else:
            base, low = call(local_kernel, [field, low_out], [u, rhs, matrix])
        if sweep + 1 < SWEEPS:
            residual, chunk = call(
                residual_kernel,
                [field, far_out((peers, rights, count), BF16)],
                [tables, masks, base, basis, *arrived],
            )
        else:
            (left,) = call(
                last_kernel, [far_out((rights, order), BF16)], [tables, masks, base, *arrived]
            )
    return low.T[None, None], left.T[None, None]


def solution(mesh):
    placed = (
        P("sub", "reg", None, None),
        P("sub", "reg", None, None, None),
        P("sub", "reg", None, None),
        P("sub", "reg", None),
        P("sub", "reg", None),
        P("sub", "reg", None, None),
        P("sub", "reg", None, None),
        P("sub", "reg", None),
        P("reg", "sub", None),
    )
    return jax.shard_map(
        body,
        mesh=mesh,
        in_specs=placed,
        out_specs=(P("sub", "reg", None, None), P("sub", "reg", None, None)),
        check_vma=False,
    )
```
